32 devices in a mesh: wave: 8 (over y, x, core), lev: 4 (over z).
Axes of the slice: x: 2, y: 2, z: 4, core: 2. Of those that a mesh axis runs over, the one named last changes fastest.
Arguments:
- coefficients: bfloat16 [640, 640, 512], P('wave', 'lev'), may hold values from -6 to 6
- factors: bfloat16 [3, 2, 640, 80, 640], P(None, None, 'wave', None, 'lev'), may hold values from -0.5 to 0.5
- wave_ids: int32 [640], replicated, may hold values from 0 to 639, each once
Outputs:
- grid: bfloat16 [640, 256, 2560], P(('wave', 'lev'))
The draws below stay inside these ranges and needn't reach their ends.
Inputs may be any that keep to these rules, and one draw needn't show every extreme that they name: `wave_ids`: each wavenumber 0 .. 639 appears exactly once.
All inputs are finite; a program needn't handle non-finite values.
Results may differ from the reference program's by a relative error of at most 0.0079.
Values may be sent and summed in bfloat16 or wider, within the bound.
A program may use at most 192 MiB of HBM per device.

```python
import math
import jax
import jax.numpy as jnp
from jax import lax

NDEG = 640
WAVES = 640
NLON = 2560
FIELDS = 8
LEVELS = 32
SECTIONS = 3
N_WAVE = 8
N_LEV = 4


def block_scale(rng, extent, shards, least, largest):
    gain = 1.0
    for position, shards_of in shards:
        draws = jax.random.uniform(jax.random.fold_in(jax.random.fold_in(rng, 6), position), (shards_of,), jnp.float32, least / len(shards), largest / len(shards))
        gain = gain * jnp.repeat(jnp.exp(draws), extent[position] // shards_of).reshape((-1,) + (1,) * (len(extent) - 1 - position))
    return gain


def noise(own_key, dims, scale, reach, cuts=(), held_as=jnp.bfloat16):
    array = jax.random.normal(own_key, dims, jnp.float32) * scale
    if len(cuts) > 0:
        array = block_scale(own_key, dims, cuts, -0.22, 0.18) * array
    return jnp.clip(array, min=-reach, max=reach).astype(held_as)


def setup_inputs(seed: int = 0) -> dict:
    arg_keys = jax.random.split(jax.random.key(seed), 4)
    return {
        "coefficients": noise(arg_keys[0], (NDEG, WAVES, 2 * FIELDS * LEVELS), 1.0, 6.0, ((0, 8), (1, 4))),
        "factors": noise(arg_keys[1], (SECTIONS, 2, NDEG, NDEG // N_WAVE, WAVES), (2 * NDEG // N_WAVE) ** -0.5, 0.5, ((2, 8), (4, 4))),
        "wave_ids": jax.random.permutation(arg_keys[2], WAVES).astype(jnp.int32),
    }


def reference(coefficients, factors, wave_ids):
    deg_block = NDEG // N_WAVE
    wave_block = WAVES // N_LEV
    channels = 2 * FIELDS * LEVELS
    degree = jnp.arange(NDEG, dtype=jnp.int32)

    def synthesize(block_index):
        offset = (block_index * wave_block).astype(jnp.int32)
        coef_block = lax.dynamic_slice_in_dim(coefficients, offset, wave_block, 1)
        own_ids = lax.dynamic_slice_in_dim(wave_ids, offset, wave_block, 0)
        live_mask = (degree[:, None] >= own_ids[None, :])[:, :, None]
        current = jnp.where(live_mask, coef_block, jnp.zeros((), coefficients.dtype))
        for section in range(SECTIONS):
            stride = 1 << section
            section_factors = lax.dynamic_slice_in_dim(factors[section], offset, wave_block, 3).astype(jnp.float32)
            self_factor = section_factors[0].reshape(N_WAVE, deg_block, deg_block, wave_block)
            partner_factor = section_factors[1].reshape(N_WAVE, deg_block, deg_block, wave_block)
            blocks_now = current.astype(jnp.float32).reshape(N_WAVE, deg_block, wave_block, channels)
            partner = blocks_now.reshape(N_WAVE // (2 * stride), 2, stride, deg_block, wave_block, channels)[:, ::-1]
            partner = partner.reshape(blocks_now.shape)
            combined = jnp.einsum('woim,wimc->womc', self_factor, blocks_now)
            combined = combined + jnp.einsum('woim,wimc->womc', partner_factor, partner)
            current = combined.reshape(NDEG, wave_block, channels).astype(jnp.bfloat16)
        return current
    blocks = lax.map(synthesize, jnp.arange(N_LEV, dtype=jnp.int32))
    lat_rows = jnp.transpose(blocks, (1, 0, 2, 3)).reshape(NDEG, WAVES, 2, FIELDS * LEVELS)
    longitude = jnp.arange(NLON, dtype=jnp.int32)
    phases = wave_ids[:, None] * longitude[None, :] % NLON
    angles = phases.astype(jnp.float32) * (2.0 * math.pi / NLON)
    weight = jnp.where(wave_ids == 0, 1.0, 2.0).astype(jnp.float32) / math.sqrt(2.0 * WAVES)
    cosine_part = weight[:, None] * jnp.cos(angles)
    sine_part = -weight[:, None] * jnp.sin(angles)
    fourier_table = jnp.stack([cosine_part, sine_part], axis=1).astype(jnp.bfloat16).astype(jnp.float32)
    lat_block = math.gcd(NDEG, 64)

    def fourier(block_index):
        offset = (block_index * lat_block).astype(jnp.int32)
        piece = lax.dynamic_slice_in_dim(lat_rows, offset, lat_block, 0).astype(jnp.float32)
        return jnp.einsum('rmpc,mpj->rcj', piece, fourier_table).astype(jnp.bfloat16)
    grid = lax.map(fourier, jnp.arange(NDEG // lat_block, dtype=jnp.int32))
    return grid.reshape(NDEG, FIELDS * LEVELS, NLON)
```

```python
import functools
import math

import jax
import jax.numpy as jnp
from jax import lax
from jax.experimental import pallas as pl
from jax.experimental.pallas import tpu as pltpu
from jax.sharding import PartitionSpec as P

NLON = 2560


def swapped(block, axis, apart):
    count = lax.axis_size(axis)
    route = []
    for low in range(count):
        high = low | 1 << apart
        if high != low and high < count:
            route += [(low, high), (high, low)]
    return lax.ppermute(block, axis, route)


def combine_kernel(count, factor_ref, own_ref, partner_ref, *refs):
    out_ref = refs[-1]
    for m in range(count):
        total = jnp.dot(factor_ref[0, m], own_ref[m], preferred_element_type=jnp.float32)
        total += jnp.dot(factor_ref[1, m], partner_ref[m], preferred_element_type=jnp.float32)
        out_ref[m] = total.astype(out_ref.dtype)


def combine(factor, own, partner, start, after):
    slots, rows, channels = own.shape
    step = math.gcd(slots, 8)
    block = pl.BlockSpec((step, rows, channels), lambda i: (i, 0, 0))
    return pl.pallas_call(
        functools.partial(combine_kernel, step),
        grid=(slots // step,),
        out_shape=jax.ShapeDtypeStruct(own.shape, own.dtype),
        in_specs=[
            pl.BlockSpec((2, step, rows, rows), lambda i: (0, start // step + i, 0, 0)),
            block,
            block,
        ]
        + [pl.BlockSpec(memory_space=pl.ANY)] * len(after),
        out_specs=block,
        cost_estimate=pl.CostEstimate(
            flops=4 * slots * rows * rows * channels,
            bytes_accessed=2 * (3 * own.size + 2 * slots * rows * rows),
            transcendentals=0,
        ),
    )(factor, own, partner, *after)


def synthesis_kernel(count, *refs):
    table_ref, out_ref = refs[count], refs[count + 1]
    half = out_ref.shape[1]
    wide = jnp.concatenate([ref[0] for ref in refs[:count]], axis=0)
    turned = wide.T
    spectrum = jnp.concatenate([turned[:half], turned[half:]], axis=1)
    span = math.gcd(out_ref.shape[2], 512)
    for j in range(0, out_ref.shape[2], span):
        out_ref[0, :, j : j + span] = jnp.dot(
            spectrum, table_ref[:, j : j + span], preferred_element_type=jnp.float32
        ).astype(out_ref.dtype)


def synthesis(parts, table):
    rows, _, channels = parts[0].shape
    depth, longitudes = table.shape
    return pl.pallas_call(
        functools.partial(synthesis_kernel, len(parts)),
        grid=(rows,),
        out_shape=jax.ShapeDtypeStruct((rows, channels // 2, longitudes), parts[0].dtype),
        in_specs=[pl.BlockSpec((1, p.shape[1], channels), lambda i: (i, 0, 0)) for p in parts]
        + [pl.BlockSpec((depth, longitudes), lambda i: (0, 0), pipeline_mode=pl.Buffered(1))],
        out_specs=pl.BlockSpec((1, channels // 2, longitudes), lambda i: (i, 0, 0)),
        cost_estimate=pl.CostEstimate(
            flops=rows * channels * depth * longitudes,
            bytes_accessed=rows * channels * (depth + longitudes) + 2 * table.size,
            transcendentals=0,
        ),
    )(*parts, table)


def cuts_of(slots):
    unit = math.gcd(slots, 16)
    edges = [0]
    while edges[-1] < slots:
        left = slots - edges[-1]
        edges.append(edges[-1] + (unit if edges[-1] == 0 or left <= 2 * unit else 2 * unit))
    return list(zip(edges[:-1], edges[1:]))


def body(coefficients, factors, wave_ids):
    wave_count = lax.axis_size("wave")
    lev_count = lax.axis_size("lev")
    sections = wave_count.bit_length() - 1
    rows, slots, channels = coefficients.shape
    total_waves = wave_ids.shape[0]
    wave_pos = lax.axis_index("wave")
    lev_pos = lax.axis_index("lev")
    cuts = cuts_of(slots)
    pieces = len(cuts)
    band = rows // lev_count
    ids = [
        lax.dynamic_slice_in_dim(wave_ids, (lev_pos - d) % lev_count * slots, slots, 0)
        for d in range(lev_count)
    ]
    degree = wave_pos * rows + jnp.arange(rows, dtype=jnp.int32)
    factor = [factors[s].transpose(0, 3, 1, 2) for s in range(sections)]

    current = [None] * pieces
    gathered = [None] * pieces

    def start(c):
        low, high = cuts[c]
        live = (degree[:, None] >= ids[0][low:high][None, :])[:, :, None]
        block = coefficients[:, low:high, :]
        block = jnp.where(live, block, jnp.zeros((), block.dtype))
        return block.transpose(1, 0, 2)

    def spread(c):
        ready = current[c].transpose(1, 0, 2)
        got = [lax.dynamic_slice_in_dim(ready, lev_pos * band, band, 0)]
        for d in range(1, lev_count):
            part = lax.dynamic_slice_in_dim(ready, (lev_pos + d) % lev_count * band, band, 0)
            route = [(k, (k + d) % lev_count) for k in range(lev_count)]
            got.append(lax.ppermute(part, "lev", route))
        gathered[c] = got

    for c in range(pieces):
        current[c] = start(c)
    after = []
    for t in range(pieces + sections + 1):
        for s in range(sections):
            c = t - s - (s > 0)
            if 0 <= c < pieces:
                partner = swapped(current[c], "wave", s)
                if s == sections - 1 and c >= 2:
                    after = after + gathered[c - 2][1:]
                current[c] = combine(factor[s], current[c], partner, cuts[c][0], after)
                after = [current[c]]
                if s == sections - 1:
                    spread(c)

    table_ids = jnp.concatenate([ids[d][low:high] for low, high in cuts for d in range(lev_count)])
    longitude = jnp.arange(NLON, dtype=jnp.int32)
    phases = table_ids[:, None] * longitude[None, :] % NLON
    angles = phases.astype(jnp.float32) * (2.0 * math.pi / NLON)
    weight = jnp.where(table_ids == 0, 1.0, 2.0).astype(jnp.float32) / math.sqrt(2.0 * total_waves)
    cosine_part = (weight[:, None] * jnp.cos(angles)).astype(jnp.bfloat16)
    sine_part = (-weight[:, None] * jnp.sin(angles)).astype(jnp.bfloat16)
    table = jnp.concatenate([cosine_part, sine_part], axis=0)

    return synthesis([part for got in gathered for part in got], table)


def solution(mesh):
    in_specs = (P("wave", "lev", None), P(None, None, "wave", None, "lev"), P())
    out_specs = P(("wave", "lev"), None, None)
    return jax.shard_map(body, mesh=mesh, in_specs=in_specs, out_specs=out_specs, check_vma=False)
```

```python
import functools
import math

import jax
import jax.numpy as jnp
from jax import lax
from jax.experimental import pallas as pl
from jax.sharding import PartitionSpec as P


NLON = 2560


def swapped(block, axis, apart):
    count = lax.axis_size(axis)
    route = []
    for low in range(count):
        high = low | 1 << apart
        if high != low and high < count:
            route += [(low, high), (high, low)]
    return lax.ppermute(block, axis, route)


def combine_kernel(count, factor_ref, own_ref, partner_ref, *refs):
    out_ref = refs[-1]
    for m in range(count):
        total = jnp.dot(factor_ref[0, m], own_ref[m], preferred_element_type=jnp.float32)
        total += jnp.dot(factor_ref[1, m], partner_ref[m], preferred_element_type=jnp.float32)
        out_ref[m] = total.astype(out_ref.dtype)


def combine(factor, own, partner, start, after):
    slots, rows, channels = own.shape
    step = math.gcd(slots, 8)
    block = pl.BlockSpec((step, rows, channels), lambda i: (i, 0, 0))
    return pl.pallas_call(
        functools.partial(combine_kernel, step),
        grid=(slots // step,),
        out_shape=jax.ShapeDtypeStruct(own.shape, own.dtype),
        in_specs=[
            pl.BlockSpec((2, step, rows, rows), lambda i: (0, start // step + i, 0, 0)),
            block,
            block,
        ]
        + [pl.BlockSpec(memory_space=pl.ANY)] * len(after),
        out_specs=block,
        cost_estimate=pl.CostEstimate(
            flops=4 * slots * rows * rows * channels,
            bytes_accessed=2 * (3 * own.size + 2 * slots * rows * rows),
            transcendentals=0,
        ),
    )(factor, own, partner, *after)


def synthesis_kernel(count, *refs):
    table_ref, out_ref = refs[count], refs[count + 1]
    half = out_ref.shape[1]
    wide = jnp.concatenate([ref[0] for ref in refs[:count]], axis=0)
    turned = wide.T
    spectrum = jnp.concatenate([turned[:half], turned[half:]], axis=1)
    span = math.gcd(out_ref.shape[2], 512)
    for j in range(0, out_ref.shape[2], span):
        out_ref[0, :, j : j + span] = jnp.dot(
            spectrum, table_ref[:, j : j + span], preferred_element_type=jnp.float32
        ).astype(out_ref.dtype)


def synthesis(parts, table):
    rows, _, channels = parts[0].shape
    depth, longitudes = table.shape
    return pl.pallas_call(
        functools.partial(synthesis_kernel, len(parts)),
        grid=(rows,),
        out_shape=jax.ShapeDtypeStruct((rows, channels // 2, longitudes), parts[0].dtype),
        in_specs=[pl.BlockSpec((1, p.shape[1], channels), lambda i: (i, 0, 0)) for p in parts]
        + [pl.BlockSpec((depth, longitudes), lambda i: (0, 0), pipeline_mode=pl.Buffered(1))],
        out_specs=pl.BlockSpec((1, channels // 2, longitudes), lambda i: (i, 0, 0)),
        cost_estimate=pl.CostEstimate(
            flops=rows * channels * depth * longitudes,
            bytes_accessed=rows * channels * (depth + longitudes) + 2 * table.size,
            transcendentals=0,
        ),
    )(*parts, table)


def cuts_of(slots):
    unit = math.gcd(slots, 16)
    edges = [0]
    while edges[-1] < slots:
        left = slots - edges[-1]
        edges.append(edges[-1] + (unit if edges[-1] == 0 or left <= 2 * unit else 2 * unit))
    return list(zip(edges[:-1], edges[1:]))


def mixes(pieces, sections):
    return [
        (t - s - (s > 0), s)
        for t in range(pieces + sections + 1)
        for s in range(sections)
        if 0 <= t - s - (s > 0) < pieces
    ]


def body(coefficients, factors, wave_ids):
    wave_count = lax.axis_size("wave")
    lev_count = lax.axis_size("lev")
    sections = wave_count.bit_length() - 1
    rows, slots, _ = coefficients.shape
    total_waves = wave_ids.shape[0]
    wave_pos = lax.axis_index("wave")
    lev_pos = lax.axis_index("lev")
    cuts = cuts_of(slots)
    pieces = len(cuts)
    band = rows // lev_count
    ids = [
        lax.dynamic_slice_in_dim(wave_ids, (lev_pos - d) % lev_count * slots, slots, 0)
        for d in range(lev_count)
    ]
    degree = wave_pos * rows + jnp.arange(rows, dtype=jnp.int32)
    factor = [factors[s].transpose(0, 3, 1, 2) for s in range(sections)]

    current = [None] * pieces
    gathered = [None] * pieces

    def start(c):
        low, high = cuts[c]
        live = (degree[:, None] >= ids[0][low:high][None, :])[:, :, None]
        block = coefficients[:, low:high, :]
        block = jnp.where(live, block, jnp.zeros((), block.dtype))
        return block.transpose(1, 0, 2)

    def spread(c):
        ready = current[c].transpose(1, 0, 2)
        got = [lax.dynamic_slice_in_dim(ready, lev_pos * band, band, 0)]
        for d in range(1, lev_count):
            part = lax.dynamic_slice_in_dim(ready, (lev_pos + d) % lev_count * band, band, 0)
            route = [(k, (k + d) % lev_count) for k in range(lev_count)]
            got.append(lax.ppermute(part, "lev", route))
        gathered[c] = got

    for c in range(pieces):
        current[c] = start(c)
    after = []
    for c, s in mixes(pieces, sections):
        partner = swapped(current[c], "wave", s)
        current[c] = combine(factor[s], current[c], partner, cuts[c][0], after)
        after = [current[c]]
        if s == sections - 1:
            spread(c)

    table_ids = jnp.concatenate([ids[d][low:high] for low, high in cuts for d in range(lev_count)])
    longitude = jnp.arange(NLON, dtype=jnp.int32)
    phases = table_ids[:, None] * longitude[None, :] % NLON
    angles = phases.astype(jnp.float32) * (2.0 * math.pi / NLON)
    weight = jnp.where(table_ids == 0, 1.0, 2.0).astype(jnp.float32) / math.sqrt(2.0 * total_waves)
    cosine_part = (weight[:, None] * jnp.cos(angles)).astype(jnp.bfloat16)
    sine_part = (-weight[:, None] * jnp.sin(angles)).astype(jnp.bfloat16)
    table = jnp.concatenate([cosine_part, sine_part], axis=0)

    return synthesis([part for got in gathered for part in got], table)


def solution(mesh):
    in_specs = (P("wave", "lev", None), P(None, None, "wave", None, "lev"), P())
    out_specs = P(("wave", "lev"), None, None)
    return jax.shard_map(body, mesh=mesh, in_specs=in_specs, out_specs=out_specs, check_vma=False)
```
